32 devices in a mesh: feat: 16 (over z, y, x), tok: 2 (over core).
Axes of the slice: x: 2, y: 2, z: 4, core: 2. Of those that a mesh axis runs over, the one named last changes fastest.
Arguments:
- tokens: bfloat16 [128, 4, 8192], P('feat', None, 'tok'), may hold values from -6 to 6
- gate_weight: bfloat16 [8192, 28672], P('tok', 'feat'), may hold values from -0.0625 to 0.0625
- up_weight: bfloat16 [8192, 28672], P('tok', 'feat'), may hold values from -0.0625 to 0.0625
- down_weight: bfloat16 [28672, 8192], P('feat', 'tok'), may hold values from -0.03125 to 0.03125
- alignment: int32 [3, 128], replicated, may hold values from 0 to 127, each once within a row
Outputs:
- ffn_out: bfloat16 [128, 4, 8192], P('feat', None, 'tok')
- cross: float32 [3, 8192, 8192], P(None, 'feat', 'tok')
The draws below stay inside these ranges and needn't reach their ends.
Inputs may be any that keep to these rules, and one draw needn't show every extreme that they name: Each row of alignment holds every token index 0 .. 127 exactly once.
All inputs are finite; a program needn't handle non-finite values.
Results may differ from the reference program's by a relative error of at most 0.025.
Values may be sent and summed in bfloat16 or wider, within the bound.
No kernel may reach another device: no remote copies, remote signals or barrier semaphores. Data moves between devices by JAX's collectives and lax.ppermute only.
A program may use at most 192 MiB of HBM per device.

```python
import math
import jax
import jax.numpy as jnp
from jax import lax

D = 8192
FF = 28672
LANGS = 4
TOK_LANG = 128
N_FEAT = 16
N_TOK = 2


def levels(rng, dims, split, smallest, high):
    level, own = 1.0, jax.random.fold_in(rng, 6)
    for axis_at, shards_of in split:
        draws = jnp.exp(jax.random.uniform(jax.random.fold_in(own, axis_at), (shards_of,), jnp.float32, smallest / len(split), high / len(split)))
        level = level * jnp.repeat(draws, dims[axis_at] // shards_of).reshape([-1 if axis == axis_at else 1 for axis in range(len(dims))])
    return level


def normal_values(key, extent, deviation, reach, shards=(), kind=jnp.bfloat16):
    drawn = jax.random.normal(key, extent, jnp.float32) * deviation
    if len(shards) > 0:
        drawn = levels(key, extent, shards, -0.22, 0.18) * drawn
    return jnp.clip(drawn, min=-reach, max=reach).astype(kind)


def setup_inputs(seed: int = 0) -> dict:
    splits = jax.random.split(jax.random.key(seed), 6)
    return {
        "tokens": normal_values(splits[0], (TOK_LANG, LANGS, D), 1.0, 6.0, ((0, 16), (2, 2))),
        "gate_weight": normal_values(splits[1], (D, FF), D ** -0.5, 0.0625, ((0, 2), (1, 16))),
        "up_weight": normal_values(splits[2], (D, FF), D ** -0.5, 0.0625, ((0, 2), (1, 16))),
        "down_weight": normal_values(splits[3], (FF, D), FF ** -0.5, 0.03125, ((0, 16), (1, 2))),
        "alignment": jax.vmap(lambda own: jax.random.permutation(own, TOK_LANG))(jax.random.split(splits[4], (LANGS - 1))).reshape((LANGS - 1, TOK_LANG)).astype(jnp.int32),
    }


def reference(tokens, gate_weight, up_weight, down_weight, alignment):
    flattened = tokens.reshape(TOK_LANG * LANGS, D)
    width_block = D // N_TOK
    gate_vals = jnp.zeros((TOK_LANG * LANGS, FF), jnp.float32)
    up_vals = jnp.zeros((TOK_LANG * LANGS, FF), jnp.float32)
    for block in range(N_TOK):
        piece = flattened[:, block * width_block:(block + 1) * width_block]
        gate_part = jnp.dot(piece, gate_weight[block * width_block:(block + 1) * width_block], preferred_element_type=jnp.float32)
        up_part = jnp.dot(piece, up_weight[block * width_block:(block + 1) * width_block], preferred_element_type=jnp.float32)
        gate_vals = gate_vals + lax.optimization_barrier(gate_part.astype(jnp.bfloat16)).astype(jnp.float32)
        up_vals = up_vals + lax.optimization_barrier(up_part.astype(jnp.bfloat16)).astype(jnp.float32)
    hidden = (jax.nn.silu(gate_vals) * up_vals).astype(jnp.bfloat16)
    hidden_block = FF // N_FEAT
    summed = jnp.zeros((TOK_LANG * LANGS, D), jnp.float32)
    for block in range(N_FEAT):
        out_part = jnp.dot(hidden[:, block * hidden_block:(block + 1) * hidden_block], down_weight[block * hidden_block:(block + 1) * hidden_block], preferred_element_type=jnp.float32)
        summed = summed + lax.optimization_barrier(out_part.astype(jnp.bfloat16)).astype(jnp.float32)
    ffn_out = summed.astype(jnp.bfloat16).reshape(TOK_LANG, LANGS, D)
    english = ffn_out[:, 0, :]
    scaling = 1.0 / math.sqrt(TOK_LANG)
    blocks = []
    for language in range(1, LANGS):
        other_rows = jnp.take(ffn_out[:, language, :], alignment[language - 1], axis=0)
        product = lax.dot_general(english, other_rows, (((0,), (0,)), ((), ())), preferred_element_type=jnp.float32)
        blocks.append(product * scaling)
    return (ffn_out, jnp.stack(blocks))
```

```python
import math

import jax
import jax.numpy as jnp
import numpy as np
from jax import lax
from jax.sharding import PartitionSpec as P

BF16 = jnp.bfloat16
F32 = jnp.float32


def feat_shape(n):
    if n == 16:
        return 4, 2, 2
    if n == 32:
        return 2, 4, 4
    return 1, 1, n


def folded(n):
    return list(range(0, n, 2)) + list(range(1, n, 2))[::-1]


def plane_cycle(ny, nx):
    if ny < 2 or nx < 2:
        return folded(ny * nx)
    cycle = [(0, x) for x in range(nx)]
    for y in range(1, ny):
        xs = range(1, nx) if y % 2 == 0 else range(nx - 1, 0, -1)
        cycle += [(y, x) for x in xs]
    cycle += [(y, 0) for y in range(ny - 1, 0, -1)]
    return [y * nx + x for y, x in cycle]


class Rings:
    def __init__(self, n_feat, n_tok):
        nz, ny, nx = feat_shape(n_feat)
        self.n_feat, self.n_tok = n_feat, n_tok
        self.nz, self.npl = nz, ny * nx
        self.zorder = folded(nz)
        self.porder = plane_cycle(ny, nx)
        self.zpos = {z: i for i, z in enumerate(self.zorder)}
        self.ppos = {p: i for i, p in enumerate(self.porder)}

    def source(self, f, t, j, i):
        sign = 1 if t % 2 == 0 else -1
        z, p = divmod(f, self.npl)
        z2 = self.zorder[(self.zpos[z] - i) % self.nz]
        p2 = self.porder[(self.ppos[p] - sign * j) % self.npl]
        return z2 * self.npl + p2

    def perm(self, which, back):
        pairs = []
        for f in range(self.n_feat):
            for t in range(self.n_tok):
                j, i = (1, 0) if which == "p" else (0, 1)
                s = self.source(f, t, j, i)
                pair = (s * self.n_tok + t, f * self.n_tok + t)
                pairs.append(pair[::-1] if back else pair)
        return sorted(pairs)

    def size(self, which):
        return self.npl if which == "p" else self.nz

    def gather(self, x, which):
        perm = self.perm(which, False)
        out = [x]
        for _ in range(self.size(which) - 1):
            out.append(lax.ppermute(out[-1], ("feat", "tok"), perm))
        return out

    def scatter(self, parts, which):
        perm = self.perm(which, True)
        acc = parts[-1]
        for part in parts[-2::-1]:
            got = lax.ppermute(acc, ("feat", "tok"), perm)
            acc = (got.astype(F32) + part.astype(F32)).astype(BF16)
        return acc


def mirror(n):
    return [(n - j) % n for j in range(n)]


def on_device(tokens, gate_weight, up_weight, down_weight, alignment):
    n_feat, n_tok = lax.axis_size("feat"), lax.axis_size("tok")
    rings = Rings(n_feat, n_tok)
    nz, npl = rings.nz, rings.npl
    own, langs, width = tokens.shape
    rows = own * langs
    hid = gate_weight.shape[1]
    f, t = lax.axis_index("feat"), lax.axis_index("tok")
    cut = max(width * 21 // 32 // 128 * 128, 128)

    x = tokens.transpose(1, 0, 2).reshape(rows, width)

    a = jnp.concatenate(rings.gather(x[:, :cut], "z"), 0)
    a = jnp.concatenate(rings.gather(a, "p"), 0)
    b = jnp.concatenate(rings.gather(x[:, cut:], "p"), 0)
    b = jnp.concatenate(rings.gather(b, "z"), 0)
    b = b.reshape(nz, npl, rows, width - cut).transpose(1, 0, 2, 3).reshape(-1, width - cut)
    full = jnp.concatenate((a, b), 1)

    gate = jnp.dot(full, gate_weight, preferred_element_type=F32).astype(BF16)
    up = jnp.dot(full, up_weight, preferred_element_type=F32).astype(BF16)

    def over_tok(v):
        v = v.reshape(npl, nz * rows, hid)
        flip = [v[j] for j in mirror(npl)]
        if n_tok == 2:
            other = lax.ppermute(v, "tok", [(0, 1), (1, 0)])
            other = jnp.stack([other[j] for j in mirror(npl)])
            return v.astype(F32) + other.astype(F32)
        odd = t % 2 == 1
        v = jnp.where(odd, jnp.stack(flip), v)
        total = lax.psum(v, "tok").astype(F32)
        return jnp.where(odd, jnp.stack([total[j] for j in mirror(npl)]), total)

    hidden = (jax.nn.silu(over_tok(gate)) * over_tok(up)).astype(BF16)
    hidden = hidden.reshape(-1, hid)

    oa = jnp.dot(hidden, down_weight[:, :cut], preferred_element_type=F32).astype(BF16)
    ob = jnp.dot(hidden, down_weight[:, cut:], preferred_element_type=F32).astype(BF16)

    oa = oa.reshape(npl, nz * rows, cut)
    oa = rings.scatter([oa[j] for j in range(npl)], "p").reshape(nz, rows, cut)
    oa = rings.scatter([oa[i] for i in range(nz)], "z")
    ob = ob.reshape(npl, nz, rows, width - cut)
    ob = rings.scatter([ob[:, i].reshape(npl * rows, -1) for i in range(nz)], "z")
    ob = ob.reshape(npl, rows, width - cut)
    ob = rings.scatter([ob[j] for j in range(npl)], "p")

    ffn_out = jnp.concatenate((oa, ob), 1).reshape(langs, own, width).transpose(1, 0, 2)

    a = jnp.stack(rings.gather(oa.reshape(langs, own, cut), "z"), 1)
    a = a.reshape(langs, nz * own, cut)
    a = jnp.stack(rings.gather(a, "p"), 1).reshape(langs, -1, cut)
    b = jnp.stack(rings.gather(ob.reshape(langs, own, width - cut), "p"), 1)
    b = b.reshape(langs, npl * own, width - cut)
    b = jnp.stack(rings.gather(b, "z"), 1)
    b = b.reshape(langs, nz, npl, own, width - cut).transpose(0, 2, 1, 3, 4)
    b = b.reshape(langs, -1, width - cut)
    out_all = jnp.concatenate((a, b), 2)

    ids = np.zeros((n_feat, n_tok, npl, nz, own), np.int32)
    for ff in range(n_feat):
        for tt in range(n_tok):
            for j in range(npl):
                for i in range(nz):
                    ids[ff, tt, j, i] = rings.source(ff, tt, j, i) * own + np.arange(own)
    ids = jnp.asarray(ids.reshape(n_feat * n_tok, -1))
    mine = lax.dynamic_index_in_dim(ids, f * n_tok + t, 0, keepdims=False)

    ratio = n_feat // n_tok
    fw = width // ratio
    own_block = lax.dynamic_slice_in_dim(out_all[0], f % ratio * fw, fw, 1)
    root = f // ratio
    if n_tok == 2:
        other = lax.ppermute(own_block, "tok", [(0, 1), (1, 0)])
        other = other.reshape(npl, nz * own, fw)
        other = jnp.stack([other[j] for j in mirror(npl)]).reshape(-1, fw)
        english = jnp.where(root == t, own_block, other)
    else:
        def flip(v):
            v = v.reshape(npl, nz * own, fw)
            return jnp.stack([v[j] for j in mirror(npl)]).reshape(-1, fw)

        odd = t % 2 == 1
        block = jnp.where(odd, flip(own_block), own_block)
        block = lax.psum(jnp.where(root == t, block, jnp.zeros_like(block)), "tok")
        english = jnp.where(odd, flip(block), block)

    targets = jnp.take(alignment, mine, axis=1)
    onehot = (mine[None, :, None] == targets[:, None, :]).astype(BF16)
    moved = jnp.einsum("lri,ic->lrc", onehot, english, preferred_element_type=F32).astype(BF16)
    scaling = 1.0 / math.sqrt(own * n_feat)
    cross = jnp.einsum("lrc,lrd->lcd", moved, out_all[1:], preferred_element_type=F32) * scaling
    return ffn_out, cross


def solution(mesh):
    in_specs = (P("feat", None, "tok"), P("tok", "feat"), P("tok", "feat"), P("feat", "tok"), P())
    out_specs = (P("feat", None, "tok"), P(None, "feat", "tok"))
    return jax.shard_map(
        on_device, mesh=mesh, in_specs=in_specs, out_specs=out_specs, check_vma=False
    )
```

```python
import math

import jax
import jax.numpy as jnp
import numpy as np
from jax import lax
from jax.experimental import pallas as pl
from jax.experimental.pallas import tpu as pltpu
from jax.sharding import PartitionSpec as P

BF16 = jnp.bfloat16
F32 = jnp.float32


def feat_shape(n):
    if n == 16:
        return 4, 2, 2
    if n == 32:
        return 2, 4, 4
    return 1, 1, n


def folded(n):
    return list(range(0, n, 2)) + list(range(1, n, 2))[::-1]


def plane_cycle(ny, nx):
    if ny < 2 or nx < 2:
        return folded(ny * nx)
    cycle = [(0, x) for x in range(nx)]
    for y in range(1, ny):
        xs = range(1, nx) if y % 2 == 0 else range(nx - 1, 0, -1)
        cycle += [(y, x) for x in xs]
    cycle += [(y, 0) for y in range(ny - 1, 0, -1)]
    return [y * nx + x for y, x in cycle]


class Rings:
    def __init__(self, n_feat, n_tok):
        nz, ny, nx = feat_shape(n_feat)
        self.n_feat, self.n_tok = n_feat, n_tok
        self.nz, self.npl = nz, ny * nx
        self.zorder = folded(nz)
        self.porder = plane_cycle(ny, nx)
        self.zpos = {z: i for i, z in enumerate(self.zorder)}
        self.ppos = {p: i for i, p in enumerate(self.porder)}

    def source(self, f, t, j, i):
        sign = 1 if t % 2 == 0 else -1
        z, p = divmod(f, self.npl)
        z2 = self.zorder[(self.zpos[z] - i) % self.nz]
        p2 = self.porder[(self.ppos[p] - sign * j) % self.npl]
        return z2 * self.npl + p2

    def perm(self, which, back):
        pairs = []
        for f in range(self.n_feat):
            for t in range(self.n_tok):
                j, i = (1, 0) if which == "p" else (0, 1)
                s = self.source(f, t, j, i)
                pair = (s * self.n_tok + t, f * self.n_tok + t)
                pairs.append(pair[::-1] if back else pair)
        return sorted(pairs)

    def size(self, which):
        return self.npl if which == "p" else self.nz

    def step(self, x, which, back=False):
        return lax.ppermute(x, ("feat", "tok"), self.perm(which, back))

    def gather(self, a, b, wa, wb):
        a, b = [a], [b]
        for k in range(1, max(self.size(wa), self.size(wb))):
            if k < self.size(wa):
                a.append(self.step(a[-1], wa))
            if k < self.size(wb):
                b.append(self.step(b[-1], wb))
            a[-1], b[-1] = lax.optimization_barrier((a[-1], b[-1]))
        return a, b

    def scatter(self, parts_a, parts_b, wa, wb, source):
        ja, jb = self.size(wa) - 1, self.size(wb) - 1
        a, b = parts_a(source, ja), parts_b(source, jb)
        while ja or jb:
            a, b, source = lax.optimization_barrier((a, b, source))
            got = [self.step(a, wa, True) if ja else a, self.step(b, wb, True) if jb else b]
            more = [parts_a(source, ja - 1) if ja else None, parts_b(source, jb - 1) if jb else None]
            got, more = lax.optimization_barrier((got, more))
            a, b = (
                g if m is None else (g.astype(F32) + m.astype(F32)).astype(BF16)
                for g, m in zip(got, more)
            )
            ja, jb = max(ja - 1, 0), max(jb - 1, 0)
        return a, b


def mirror(n):
    return [(n - j) % n for j in range(n)]


def on_any(tokens, gate_weight, up_weight, down_weight, alignment):
    n_feat, n_tok = lax.axis_size("feat"), lax.axis_size("tok")
    rings = Rings(n_feat, n_tok)
    nz, npl = rings.nz, rings.npl
    own, langs, width = tokens.shape
    rows = own * langs
    hid = gate_weight.shape[1]
    f, t = lax.axis_index("feat"), lax.axis_index("tok")
    cut = max(width * 21 // 32 // 128 * 128, 128)

    x = tokens.transpose(1, 0, 2).reshape(rows, width)

    a, b = rings.gather(x[:, :cut], x[:, cut:], "z", "p")
    a, b = rings.gather(jnp.concatenate(a, 0), jnp.concatenate(b, 0), "p", "z")
    a, b = jnp.concatenate(a, 0), jnp.concatenate(b, 0)
    b = b.reshape(nz, npl, rows, width - cut).transpose(1, 0, 2, 3).reshape(-1, width - cut)
    full = jnp.concatenate((a, b), 1)

    gate = jnp.dot(full, gate_weight, preferred_element_type=F32).astype(BF16)
    up = jnp.dot(full, up_weight, preferred_element_type=F32).astype(BF16)

    def over_tok(v):
        v = v.reshape(npl, nz * rows, hid)
        flip = [v[j] for j in mirror(npl)]
        if n_tok == 2:
            other = lax.ppermute(v, "tok", [(0, 1), (1, 0)])
            other = jnp.stack([other[j] for j in mirror(npl)])
            return v.astype(F32) + other.astype(F32)
        odd = t % 2 == 1
        v = jnp.where(odd, jnp.stack(flip), v)
        total = lax.psum(v, "tok").astype(F32)
        return jnp.where(odd, jnp.stack([total[j] for j in mirror(npl)]), total)

    hidden = (jax.nn.silu(over_tok(gate)) * over_tok(up)).astype(BF16)
    hidden = hidden.reshape(-1, hid)

    def down_a(h, j):
        h = h.reshape(npl, -1, hid)[j]
        return jnp.dot(h, down_weight[:, :cut], preferred_element_type=F32).astype(BF16)

    def down_b(h, i):
        h = h.reshape(npl, nz, rows, hid)[:, i].reshape(-1, hid)
        return jnp.dot(h, down_weight[:, cut:], preferred_element_type=F32).astype(BF16)

    oa, ob = rings.scatter(down_a, down_b, "p", "z", hidden)
    oa, ob = oa.reshape(nz, rows, cut), ob.reshape(npl, rows, width - cut)
    oa, ob = rings.scatter(lambda s, j: s[0][j], lambda s, j: s[1][j], "z", "p", (oa, ob))

    ffn_out = jnp.concatenate((oa, ob), 1).reshape(langs, own, width).transpose(1, 0, 2)

    a, b = oa.reshape(langs, own, cut), ob.reshape(langs, own, width - cut)
    a, b = rings.gather(a, b, "z", "p")
    a = jnp.stack(a, 1).reshape(langs, nz * own, cut)
    b = jnp.stack(b, 1).reshape(langs, npl * own, width - cut)
    a, b = rings.gather(a, b, "p", "z")
    a = jnp.stack(a, 1).reshape(langs, -1, cut)
    b = jnp.stack(b, 1)
    b = b.reshape(langs, nz, npl, own, width - cut).transpose(0, 2, 1, 3, 4)
    b = b.reshape(langs, -1, width - cut)
    out_all = jnp.concatenate((a, b), 2)

    ids = np.zeros((n_feat, n_tok, npl, nz, own), np.int32)
    for ff in range(n_feat):
        for tt in range(n_tok):
            for j in range(npl):
                for i in range(nz):
                    ids[ff, tt, j, i] = rings.source(ff, tt, j, i) * own + np.arange(own)
    ids = jnp.asarray(ids.reshape(n_feat * n_tok, -1))
    mine = lax.dynamic_index_in_dim(ids, f * n_tok + t, 0, keepdims=False)

    ratio = n_feat // n_tok
    fw = width // ratio
    own_block = lax.dynamic_slice_in_dim(out_all[0], f % ratio * fw, fw, 1)
    root = f // ratio
    if n_tok == 2:
        other = lax.ppermute(own_block, "tok", [(0, 1), (1, 0)])
        other = other.reshape(npl, nz * own, fw)
        other = jnp.stack([other[j] for j in mirror(npl)]).reshape(-1, fw)
        english = jnp.where(root == t, own_block, other)
    else:
        def flip(v):
            v = v.reshape(npl, nz * own, fw)
            return jnp.stack([v[j] for j in mirror(npl)]).reshape(-1, fw)

        odd = t % 2 == 1
        block = jnp.where(odd, flip(own_block), own_block)
        block = lax.psum(jnp.where(root == t, block, jnp.zeros_like(block)), "tok")
        english = jnp.where(odd, flip(block), block)

    targets = jnp.take(alignment, mine, axis=1)
    onehot = (mine[None, :, None] == targets[:, None, :]).astype(BF16)
    moved = jnp.einsum("lri,ic->lrc", onehot, english, preferred_element_type=F32).astype(BF16)
    scaling = 1.0 / math.sqrt(own * n_feat)
    cross = jnp.einsum("lrc,lrd->lcd", moved, out_all[1:], preferred_element_type=F32) * scaling
    return ffn_out, cross


class Small:
    def __init__(self):
        self.rings = Rings(16, 2)

    def mask(self, slot, t):
        one, two = slot & 1, slot >> 1
        return one + 2 * two if t == 0 else 2 * one + two

    def plane(self, x, slot):
        pairs = [(2 * f + t, 2 * (f ^ self.mask(slot, t)) + t) for f in range(16) for t in range(2)]
        return lax.ppermute(x, ("feat", "tok"), pairs)

    def z(self, x, slot=1, back=False):
        pairs = []
        for f in range(16):
            for t in range(2):
                pair = (2 * self.rings.source(f, t, 0, slot) + t, 2 * f + t)
                pairs.append(pair[::-1] if back else pair)
        return lax.ppermute(x, ("feat", "tok"), sorted(pairs))

    def tokens(self, own):
        ids = np.zeros((16, 2, 4, 4, own), np.int32)
        for f in range(16):
            for t in range(2):
                for p in range(4):
                    for i in range(4):
                        source = self.rings.source(f ^ self.mask(p, t), t, 0, i)
                        ids[f, t, p, i] = source * own + np.arange(own)
        return ids.reshape(32, -1)


def total(*parts):
    return sum(p.astype(F32) for p in parts).astype(BF16)


def cross_kernel(scaling, hot_a, hot_b, english, *refs):
    out, moved_a, moved_b = refs[8:]
    lang, step = pl.program_id(0), pl.program_id(1)
    tile = out.shape[1]

    @pl.when(step == 0)
    def _():
        for hot, moved in ((hot_a, moved_a), (hot_b, moved_b)):
            rows = jnp.dot(hot[lang], english[...], preferred_element_type=F32)
            moved[...] = rows.astype(BF16).T

    at = pl.ds(pl.multiple_of(step * tile, tile), tile)
    start = 0
    for moved, blocks in ((moved_a, refs[:4]), (moved_b, refs[4:8])):
        width = blocks[0].shape[2]
        rows = jnp.concatenate([b[lang + 1] for b in blocks], 0)
        out[0, :, start:start + width] = jnp.dot(
            moved[at, :], rows, preferred_element_type=F32
        ) * scaling
        start += width


def cross_products(hot_a, hot_b, english, a, b, scaling):
    langs, tokens, _ = hot_a.shape
    height = english.shape[1]
    width = a[0].shape[2] + b[0].shape[2]
    tile = 256
    return pl.pallas_call(
        lambda *refs: cross_kernel(scaling, *refs),
        grid=(langs, height // tile),
        in_specs=[pl.BlockSpec(memory_space=pltpu.VMEM)] * 11,
        out_specs=pl.BlockSpec((1, tile, width), lambda l, r: (l, r, 0)),
        out_shape=jax.ShapeDtypeStruct((langs, height, width), F32),
        scratch_shapes=[pltpu.VMEM((height, tokens), BF16)] * 2,
        compiler_params=pltpu.CompilerParams(
            dimension_semantics=("arbitrary", "arbitrary"), vmem_limit_bytes=16 << 20
        ),
    )(hot_a, hot_b, english, *a, *b)


def on_small(tokens, gate_weight, up_weight, down_weight, alignment):
    net = Small()
    own, langs, width = tokens.shape
    rows = own * langs
    hid = gate_weight.shape[1]
    f, t = lax.axis_index("feat"), lax.axis_index("tok")
    cut = width * 5 // 8
    lock = lax.optimization_barrier

    x = tokens.transpose(1, 0, 2).reshape(rows, width)

    a, b = x[:, :cut], x[:, cut:]
    b1, a1, b2, a2, b3, a3 = (
        net.plane(b, 1), net.z(a, 1), net.plane(b, 2), net.z(a, 3), net.plane(b, 3), None
    )
    a3 = net.z(a1, 1)
    a0 = jnp.concatenate((a, a1, a3, a2), 0)
    b0 = jnp.concatenate((b, b1, b2, b3), 0)
    a0, b0 = lock((a0, b0))
    a0, a1, b1 = lock((a0, net.plane(a0, 1), net.z(b0)))
    a0, a1, a2, b2 = lock((a0, a1, net.plane(a0, 2), net.z(b1)))
    a3, b3 = lock((net.plane(a1, 2), net.z(b2)))
    a = jnp.concatenate((a0, a1, a2, a3), 0)
    b = jnp.stack((b0, b1, b2, b3)).reshape(4, 4, rows, width - cut)
    b = b.transpose(1, 0, 2, 3).reshape(-1, width - cut)
    full = jnp.concatenate((a, b), 1)

    def core(v):
        return lax.ppermute(v, "tok", [(0, 1), (1, 0)])

    def mirror(v):
        v = v.reshape(4, -1, v.shape[-1])
        return jnp.stack((v[0], v[2], v[1], v[3])).reshape(-1, v.shape[-1])

    gate = jnp.dot(full, gate_weight, preferred_element_type=F32).astype(BF16)
    up = jnp.dot(full, up_weight, preferred_element_type=F32).astype(BF16)
    gate = gate.astype(F32) + mirror(core(gate)).astype(F32)
    up = up.astype(F32) + mirror(core(up)).astype(F32)
    hidden = (jax.nn.silu(gate) * up).astype(BF16)

    def down_a(h, j):
        h = h[j * 4 * rows:(j + 1) * 4 * rows]
        return jnp.dot(h, down_weight[:, :cut], preferred_element_type=F32).astype(BF16)

    def down_b(h, i):
        h = h.reshape(4, 4, rows, hid)[:, i].reshape(-1, hid)
        return jnp.dot(h, down_weight[:, cut:], preferred_element_type=F32).astype(BF16)

    p, q = down_a(hidden, 3), down_b(hidden, 3)
    p, q, hidden = lock((p, q, hidden))
    s3, r3 = net.plane(p, 2), net.z(q, back=True)
    p, q = down_a(hidden, 2), down_b(hidden, 2)
    s3, r3, p, q, hidden = lock((s3, r3, p, q, hidden))
    p, q, hidden = lock((p, total(q, r3), hidden))
    s2, r2 = net.plane(p, 2), net.z(q, back=True)
    p, q = down_a(hidden, 1), down_b(hidden, 1)
    s2, r2, p, q, hidden = lock((s2, r2, p, q, hidden))
    p, q, hidden = lock((total(p, s3), total(q, r2), hidden))
    s1, r1 = net.plane(p, 1), net.z(q, back=True)
    p, q = down_a(hidden, 0), down_b(hidden, 0)
    s1, r1, p, q = lock((s1, r1, p, q))
    p = total(p, s1, s2).reshape(4, rows, cut)
    q = total(q, r1).reshape(4, rows, width - cut)
    p, q = lock((p, q))
    got = lock((
        net.plane(q[1], 1), net.z(p[1], 1, True), net.plane(q[2], 2),
        net.z(p[3], 3, True), net.plane(q[3], 3), net.z(p[2], 2, True),
    ))
    p, q = lock((total(p[0], *got[1::2]), total(q[0], *got[::2])))

    ffn_out = jnp.concatenate((p, q), 1).reshape(langs, own, width).transpose(1, 0, 2)

    got = lock((
        net.plane(q, 1), net.z(p, 1), net.plane(q, 2), net.z(p, 3), net.plane(q, 3), net.z(p, 2)
    ))

    def join(*v):
        v = [x.reshape(langs, own, -1) for x in v]
        return jnp.stack(v, 1).reshape(langs, 4 * own, -1)

    p0 = join(p, got[1], got[5], got[3])
    q0 = join(q, got[0], got[2], got[4])
    p0, q0 = lock((p0, q0))
    p0, p1, q1 = lock((p0, net.plane(p0, 1), net.z(q0)))
    p0, p1, p2, q2 = lock((p0, p1, net.plane(p0, 2), net.z(q1)))
    p3, q3 = lock((net.plane(p1, 2), net.z(q2)))

    ea = jnp.concatenate((p0[0], p1[0], p2[0], p3[0]), 0)
    eb = jnp.stack((q0[0], q1[0], q2[0], q3[0])).reshape(4, 4, own, width - cut)
    eb = eb.transpose(1, 0, 2, 3).reshape(-1, width - cut)
    fw = width // 8
    block = lax.dynamic_slice_in_dim(jnp.concatenate((ea, eb), 1), f % 8 * fw, fw, 1)
    english = jnp.where(f // 8 == t, block, mirror(core(block)))

    ids = jnp.asarray(net.tokens(own))
    ids = lax.dynamic_index_in_dim(ids, f * 2 + t, 0, keepdims=False)
    targets = jnp.take(alignment, ids, axis=1)
    hot_a = (ids[None, :, None] == targets[:, None, :]).astype(BF16)
    hot_b = hot_a.reshape(-1, 4, 4, own, 16 * own).transpose(0, 2, 1, 3, 4).reshape(hot_a.shape)
    scaling = 1.0 / math.sqrt(own * 16)
    cross = cross_products(
        hot_a, hot_b, english, (p0, p1, p2, p3), (q0, q1, q2, q3), scaling
    )
    return ffn_out, cross


def solution(mesh):
    in_specs = (P("feat", None, "tok"), P("tok", "feat"), P("tok", "feat"), P("feat", "tok"), P())
    out_specs = (P("feat", None, "tok"), P(None, "feat", "tok"))
    small = mesh.shape["feat"] == 16 and mesh.shape["tok"] == 2
    body = on_small if small else on_any
    return jax.shard_map(
        body, mesh=mesh, in_specs=in_specs, out_specs=out_specs, check_vma=False
    )
```

```python
import math

import jax
import jax.numpy as jnp
import numpy as np
from jax import lax
from jax.experimental import pallas as pl
from jax.experimental.pallas import tpu as pltpu
from jax.sharding import PartitionSpec as P

BF16 = jnp.bfloat16
F32 = jnp.float32


def feat_shape(n):
    if n == 16:
        return 4, 2, 2
    if n == 32:
        return 2, 4, 4
    return 1, 1, n


def folded(n):
    return list(range(0, n, 2)) + list(range(1, n, 2))[::-1]


def plane_cycle(ny, nx):
    if ny < 2 or nx < 2:
        return folded(ny * nx)
    cycle = [(0, x) for x in range(nx)]
    for y in range(1, ny):
        xs = range(1, nx) if y % 2 == 0 else range(nx - 1, 0, -1)
        cycle += [(y, x) for x in xs]
    cycle += [(y, 0) for y in range(ny - 1, 0, -1)]
    return [y * nx + x for y, x in cycle]


class Rings:
    def __init__(self, n_feat, n_tok):
        nz, ny, nx = feat_shape(n_feat)
        self.n_feat, self.n_tok = n_feat, n_tok
        self.nz, self.npl = nz, ny * nx
        self.zorder = folded(nz)
        self.porder = plane_cycle(ny, nx)
        self.zpos = {z: i for i, z in enumerate(self.zorder)}
        self.ppos = {p: i for i, p in enumerate(self.porder)}

    def source(self, f, t, j, i):
        sign = 1 if t % 2 == 0 else -1
        z, p = divmod(f, self.npl)
        z2 = self.zorder[(self.zpos[z] - i) % self.nz]
        p2 = self.porder[(self.ppos[p] - sign * j) % self.npl]
        return z2 * self.npl + p2

    def perm(self, which, back):
        pairs = []
        for f in range(self.n_feat):
            for t in range(self.n_tok):
                j, i = (1, 0) if which == "p" else (0, 1)
                s = self.source(f, t, j, i)
                pair = (s * self.n_tok + t, f * self.n_tok + t)
                pairs.append(pair[::-1] if back else pair)
        return sorted(pairs)

    def size(self, which):
        return self.npl if which == "p" else self.nz

    def step(self, x, which, back=False):
        return lax.ppermute(x, ("feat", "tok"), self.perm(which, back))

    def gather(self, a, b, wa, wb):
        a, b = [a], [b]
        for k in range(1, max(self.size(wa), self.size(wb))):
            if k < self.size(wa):
                a.append(self.step(a[-1], wa))
            if k < self.size(wb):
                b.append(self.step(b[-1], wb))
            a[-1], b[-1] = lax.optimization_barrier((a[-1], b[-1]))
        return a, b

    def scatter(self, parts_a, parts_b, wa, wb, source):
        ja, jb = self.size(wa) - 1, self.size(wb) - 1
        a, b = parts_a(source, ja), parts_b(source, jb)
        while ja or jb:
            a, b, source = lax.optimization_barrier((a, b, source))
            got = [self.step(a, wa, True) if ja else a, self.step(b, wb, True) if jb else b]
            more = [parts_a(source, ja - 1) if ja else None, parts_b(source, jb - 1) if jb else None]
            got, more = lax.optimization_barrier((got, more))
            a, b = (
                g if m is None else (g.astype(F32) + m.astype(F32)).astype(BF16)
                for g, m in zip(got, more)
            )
            ja, jb = max(ja - 1, 0), max(jb - 1, 0)
        return a, b


def mirror(n):
    return [(n - j) % n for j in range(n)]


def on_any(tokens, gate_weight, up_weight, down_weight, alignment):
    n_feat, n_tok = lax.axis_size("feat"), lax.axis_size("tok")
    rings = Rings(n_feat, n_tok)
    nz, npl = rings.nz, rings.npl
    own, langs, width = tokens.shape
    rows = own * langs
    hid = gate_weight.shape[1]
    f, t = lax.axis_index("feat"), lax.axis_index("tok")
    cut = max(width * 21 // 32 // 128 * 128, 128)

    x = tokens.transpose(1, 0, 2).reshape(rows, width)

    a, b = rings.gather(x[:, :cut], x[:, cut:], "z", "p")
    a, b = rings.gather(jnp.concatenate(a, 0), jnp.concatenate(b, 0), "p", "z")
    a, b = jnp.concatenate(a, 0), jnp.concatenate(b, 0)
    b = b.reshape(nz, npl, rows, width - cut).transpose(1, 0, 2, 3).reshape(-1, width - cut)
    full = jnp.concatenate((a, b), 1)

    gate = jnp.dot(full, gate_weight, preferred_element_type=F32).astype(BF16)
    up = jnp.dot(full, up_weight, preferred_element_type=F32).astype(BF16)

    def over_tok(v):
        v = v.reshape(npl, nz * rows, hid)
        flip = [v[j] for j in mirror(npl)]
        if n_tok == 2:
            other = lax.ppermute(v, "tok", [(0, 1), (1, 0)])
            other = jnp.stack([other[j] for j in mirror(npl)])
            return v.astype(F32) + other.astype(F32)
        odd = t % 2 == 1
        v = jnp.where(odd, jnp.stack(flip), v)
        total = lax.psum(v, "tok").astype(F32)
        return jnp.where(odd, jnp.stack([total[j] for j in mirror(npl)]), total)

    hidden = (jax.nn.silu(over_tok(gate)) * over_tok(up)).astype(BF16)
    hidden = hidden.reshape(-1, hid)

    def down_a(h, j):
        h = h.reshape(npl, -1, hid)[j]
        return jnp.dot(h, down_weight[:, :cut], preferred_element_type=F32).astype(BF16)

    def down_b(h, i):
        h = h.reshape(npl, nz, rows, hid)[:, i].reshape(-1, hid)
        return jnp.dot(h, down_weight[:, cut:], preferred_element_type=F32).astype(BF16)

    oa, ob = rings.scatter(down_a, down_b, "p", "z", hidden)
    oa, ob = oa.reshape(nz, rows, cut), ob.reshape(npl, rows, width - cut)
    oa, ob = rings.scatter(lambda s, j: s[0][j], lambda s, j: s[1][j], "z", "p", (oa, ob))

    ffn_out = jnp.concatenate((oa, ob), 1).reshape(langs, own, width).transpose(1, 0, 2)

    a, b = oa.reshape(langs, own, cut), ob.reshape(langs, own, width - cut)
    a, b = rings.gather(a, b, "z", "p")
    a = jnp.stack(a, 1).reshape(langs, nz * own, cut)
    b = jnp.stack(b, 1).reshape(langs, npl * own, width - cut)
    a, b = rings.gather(a, b, "p", "z")
    a = jnp.stack(a, 1).reshape(langs, -1, cut)
    b = jnp.stack(b, 1)
    b = b.reshape(langs, nz, npl, own, width - cut).transpose(0, 2, 1, 3, 4)
    b = b.reshape(langs, -1, width - cut)
    out_all = jnp.concatenate((a, b), 2)

    ids = np.zeros((n_feat, n_tok, npl, nz, own), np.int32)
    for ff in range(n_feat):
        for tt in range(n_tok):
            for j in range(npl):
                for i in range(nz):
                    ids[ff, tt, j, i] = rings.source(ff, tt, j, i) * own + np.arange(own)
    ids = jnp.asarray(ids.reshape(n_feat * n_tok, -1))
    mine = lax.dynamic_index_in_dim(ids, f * n_tok + t, 0, keepdims=False)

    ratio = n_feat // n_tok
    fw = width // ratio
    own_block = lax.dynamic_slice_in_dim(out_all[0], f % ratio * fw, fw, 1)
    root = f // ratio
    if n_tok == 2:
        other = lax.ppermute(own_block, "tok", [(0, 1), (1, 0)])
        other = other.reshape(npl, nz * own, fw)
        other = jnp.stack([other[j] for j in mirror(npl)]).reshape(-1, fw)
        english = jnp.where(root == t, own_block, other)
    else:
        def flip(v):
            v = v.reshape(npl, nz * own, fw)
            return jnp.stack([v[j] for j in mirror(npl)]).reshape(-1, fw)

        odd = t % 2 == 1
        block = jnp.where(odd, flip(own_block), own_block)
        block = lax.psum(jnp.where(root == t, block, jnp.zeros_like(block)), "tok")
        english = jnp.where(odd, flip(block), block)

    targets = jnp.take(alignment, mine, axis=1)
    onehot = (mine[None, :, None] == targets[:, None, :]).astype(BF16)
    moved = jnp.einsum("lri,ic->lrc", onehot, english, preferred_element_type=F32).astype(BF16)
    scaling = 1.0 / math.sqrt(own * n_feat)
    cross = jnp.einsum("lrc,lrd->lcd", moved, out_all[1:], preferred_element_type=F32) * scaling
    return ffn_out, cross


class Small:
    def __init__(self):
        self.rings = Rings(16, 2)

    def mask(self, slot, t):
        one, two = slot & 1, slot >> 1
        return one + 2 * two if t == 0 else 2 * one + two

    def plane(self, x, slot):
        pairs = [(2 * f + t, 2 * (f ^ self.mask(slot, t)) + t) for f in range(16) for t in range(2)]
        return lax.ppermute(x, ("feat", "tok"), pairs)

    def z(self, x, slot=1, back=False):
        pairs = []
        for f in range(16):
            for t in range(2):
                pair = (2 * self.rings.source(f, t, 0, slot) + t, 2 * f + t)
                pairs.append(pair[::-1] if back else pair)
        return lax.ppermute(x, ("feat", "tok"), sorted(pairs))

    def tokens(self, own):
        ids = np.zeros((16, 2, 4, 4, own), np.int32)
        for f in range(16):
            for t in range(2):
                for p in range(4):
                    for i in range(4):
                        source = self.rings.source(f ^ self.mask(p, t), t, 0, i)
                        ids[f, t, p, i] = source * own + np.arange(own)
        return ids.reshape(32, -1)


def total(*parts):
    return sum(p.astype(F32) for p in parts).astype(BF16)


def early_kernel(gate_weight, up_weight, x, gate, up):
    gate[...] = jnp.dot(x[...], gate_weight[...], preferred_element_type=F32)
    up[...] = jnp.dot(x[...], up_weight[...], preferred_element_type=F32)


def late_kernel(gate_weight, up_weight, *refs):
    mids, a3, b, (gate, up, x) = refs[:6], refs[6], refs[7:11], refs[11:]
    block, cut = a3.shape
    rows = block // 4

    @pl.when(pl.program_id(0) == 0)
    def _():
        for p in range(4):
            for i in range(4):
                start = p * block + i * rows
                x[start:start + rows, :] = b[i][p * rows:(p + 1) * rows, :]

    for weight, mid, out in ((gate_weight, mids[::2], gate), (up_weight, mids[1::2], up)):
        more = jnp.dot(x[...], weight[cut:, :], preferred_element_type=F32)
        last = jnp.dot(a3[...], weight[:cut, :], preferred_element_type=F32)
        start = 0
        for part in [*mid, last]:
            end = start + part.shape[0]
            out[start:end, :] = (more[start:end] + part[...]).astype(BF16)
            start = end


TILE = 256


def early_products(x, gate_weight, up_weight):
    rows, cut = x.shape
    hid = gate_weight.shape[1]
    weight = pl.BlockSpec((cut, TILE), lambda n: (0, n))
    out = pl.BlockSpec((rows, TILE), lambda n: (0, n))
    return pl.pallas_call(
        early_kernel,
        grid=(hid // TILE,),
        in_specs=[weight] * 2 + [pl.BlockSpec(memory_space=pltpu.VMEM)],
        out_specs=[out] * 2,
        out_shape=[jax.ShapeDtypeStruct((rows, hid), F32)] * 2,
        compiler_params=pltpu.CompilerParams(
            dimension_semantics=("arbitrary",), vmem_limit_bytes=7 << 20
        ),
    )(gate_weight, up_weight, x)


def late_products(mids, a3, b, gate_weight, up_weight, first, count):
    width = gate_weight.shape[0]
    block = a3.shape[0]
    weight = pl.BlockSpec((width, TILE), lambda n: (0, n + first))
    mid = [pl.BlockSpec((m.shape[0], TILE), lambda n: (0, n + first)) for m in mids]
    out = pl.BlockSpec((4 * block, TILE), lambda n: (0, n))
    return pl.pallas_call(
        late_kernel,
        grid=(count,),
        in_specs=[weight] * 2 + mid + [pl.BlockSpec(memory_space=pltpu.VMEM)] * 5,
        out_specs=[out] * 2,
        out_shape=[jax.ShapeDtypeStruct((4 * block, count * TILE), BF16)] * 2,
        scratch_shapes=[pltpu.VMEM((4 * block, b[0].shape[1]), BF16)],
        compiler_params=pltpu.CompilerParams(
            dimension_semantics=("arbitrary",), vmem_limit_bytes=12 << 20
        ),
    )(gate_weight, up_weight, *mids, a3, *b)


def cross_kernel(scaling, hot_a, hot_b, english, *refs):
    out, moved_a, moved_b = refs[8:]
    lang, step = pl.program_id(0), pl.program_id(1)
    tile = out.shape[1]

    @pl.when(step == 0)
    def _():
        for hot, moved in ((hot_a, moved_a), (hot_b, moved_b)):
            rows = jnp.dot(hot[lang], english[...], preferred_element_type=F32)
            moved[...] = rows.astype(BF16).T

    at = pl.ds(pl.multiple_of(step * tile, tile), tile)
    start = 0
    for moved, blocks in ((moved_a, refs[:4]), (moved_b, refs[4:8])):
        width = blocks[0].shape[2]
        rows = jnp.concatenate([b[lang + 1] for b in blocks], 0)
        out[0, :, start:start + width] = jnp.dot(
            moved[at, :], rows, preferred_element_type=F32
        ) * scaling
        start += width


def cross_products(hot_a, hot_b, english, a, b, scaling):
    langs, tokens, _ = hot_a.shape
    height = english.shape[1]
    width = a[0].shape[2] + b[0].shape[2]
    tile = 256
    return pl.pallas_call(
        lambda *refs: cross_kernel(scaling, *refs),
        grid=(langs, height // tile),
        in_specs=[pl.BlockSpec(memory_space=pltpu.VMEM)] * 11,
        out_specs=pl.BlockSpec((1, tile, width), lambda l, r: (l, r, 0)),
        out_shape=jax.ShapeDtypeStruct((langs, height, width), F32),
        scratch_shapes=[pltpu.VMEM((height, tokens), BF16)] * 2,
        compiler_params=pltpu.CompilerParams(
            dimension_semantics=("arbitrary", "arbitrary"), vmem_limit_bytes=12 << 20
        ),
    )(hot_a, hot_b, english, *a, *b)


def on_small(tokens, gate_weight, up_weight, down_weight, alignment):
    net = Small()
    own, langs, width = tokens.shape
    rows = own * langs
    hid = gate_weight.shape[1]
    f, t = lax.axis_index("feat"), lax.axis_index("tok")
    cut = width * 5 // 8
    lock = lax.optimization_barrier

    x = tokens.transpose(1, 0, 2).reshape(rows, width)

    a, b = x[:, :cut], x[:, cut:]
    b1, a1, b2, a2, b3, a3 = (
        net.plane(b, 1), net.z(a, 1), net.plane(b, 2), net.z(a, 3), net.plane(b, 3), None
    )
    a3 = net.z(a1, 1)
    weights = [pltpu.with_memory_space_constraint(w, pltpu.HBM) for w in (gate_weight, up_weight)]
    b0 = jnp.concatenate((b, b1, b2, b3), 0)
    a0 = jnp.concatenate((a, a1, a3, a2), 0)
    a0, b0 = lock((a0, b0))
    a1, b1 = net.plane(a0, 1), net.z(b0)
    mids = early_products(a0, *weights)
    a0, a1, b1, mids = lock((a0, a1, b1, mids))
    a2, b2 = net.plane(a0, 2), net.z(b1)
    mids += early_products(a1, *weights)
    a0, a1, a2, b2, mids = lock((a0, a1, a2, b2, mids))
    a3, b3 = net.plane(a1, 2), net.z(b2)
    mids += early_products(a2, *weights)
    a3, b3, mids = lock((a3, b3, mids))

    def core(v):
        return lax.ppermute(v, "tok", [(0, 1), (1, 0)])

    def mirror(v):
        v = v.reshape(4, -1, v.shape[-1])
        return jnp.stack((v[0], v[2], v[1], v[3])).reshape(-1, v.shape[-1])

    tiles = hid // TILE
    early = tiles // 2 + 1
    hidden = []
    for first, count in ((0, early), (early, tiles - early)):
        gate, up = late_products(
            mids, a3, (b0, b1, b2, b3), *weights, first, count
        )
        gate = gate.astype(F32) + mirror(core(gate)).astype(F32)
        up = up.astype(F32) + mirror(core(up)).astype(F32)
        hidden.append((jax.nn.silu(gate) * up).astype(BF16))
    hidden = jnp.concatenate(hidden, 1)

    def down_a(h, j):
        h = h[j * 4 * rows:(j + 1) * 4 * rows]
        return jnp.dot(h, down_weight[:, :cut], preferred_element_type=F32).astype(BF16)

    def down_b(h, i):
        h = h.reshape(4, 4, rows, hid)[:, i].reshape(-1, hid)
        return jnp.dot(h, down_weight[:, cut:], preferred_element_type=F32).astype(BF16)

    p, q = down_a(hidden, 3), down_b(hidden, 3)
    p, q, hidden = lock((p, q, hidden))
    s3, r3 = net.plane(p, 2), net.z(q, back=True)
    p, q = down_a(hidden, 2), down_b(hidden, 2)
    s3, r3, p, q, hidden = lock((s3, r3, p, q, hidden))
    p, q, hidden = lock((p, total(q, r3), hidden))
    s2, r2 = net.plane(p, 2), net.z(q, back=True)
    p, q = down_a(hidden, 1), down_b(hidden, 1)
    s2, r2, p, q, hidden = lock((s2, r2, p, q, hidden))
    p, q, hidden = lock((total(p, s3), total(q, r2), hidden))
    s1, r1 = net.plane(p, 1), net.z(q, back=True)
    p, q = down_a(hidden, 0), down_b(hidden, 0)
    s1, r1, p, q = lock((s1, r1, p, q))
    p = total(p, s1, s2).reshape(4, rows, cut)
    q = total(q, r1).reshape(4, rows, width - cut)
    p, q = lock((p, q))
    r1, r2, r3, g1, g3, g2 = lock((
        net.plane(q[1], 1), net.plane(q[2], 2), net.plane(q[3], 3),
        net.z(p[1], 1, True), net.z(p[3], 3, True), net.z(p[2], 2, True),
    ))
    p, q = lock((total(p[0], g1, g2, g3), total(q[0], r1, r2, r3)))

    ffn_out = jnp.concatenate((p, q), 1).reshape(langs, own, width).transpose(1, 0, 2)

    r1, g1, r2, g3, r3 = net.plane(q, 1), net.z(p, 1), net.plane(q, 2), net.z(p, 3), net.plane(q, 3)
    g2 = net.z(g1, 1)

    def join(*v):
        v = [x.reshape(langs, own, -1) for x in v]
        return jnp.stack(v, 1).reshape(langs, 4 * own, -1)

    p0 = join(p, g1, g2, g3)
    q0 = join(q, r1, r2, r3)
    p0, q0 = lock((p0, q0))
    p0, p1, q1 = lock((p0, net.plane(p0, 1), net.z(q0)))
    p0, p1, p2, q2 = lock((p0, p1, net.plane(p0, 2), net.z(q1)))
    p3, q3 = lock((net.plane(p1, 2), net.z(q2)))

    ea = jnp.concatenate((p0[0], p1[0], p2[0], p3[0]), 0)
    eb = jnp.stack((q0[0], q1[0], q2[0], q3[0])).reshape(4, 4, own, width - cut)
    eb = eb.transpose(1, 0, 2, 3).reshape(-1, width - cut)
    fw = width // 8
    block = lax.dynamic_slice_in_dim(jnp.concatenate((ea, eb), 1), f % 8 * fw, fw, 1)
    english = jnp.where(f // 8 == t, block, mirror(core(block)))

    ids = jnp.asarray(net.tokens(own))
    ids = lax.dynamic_index_in_dim(ids, f * 2 + t, 0, keepdims=False)
    targets = jnp.take(alignment, ids, axis=1)
    hot_a = (ids[None, :, None] == targets[:, None, :]).astype(BF16)
    hot_b = hot_a.reshape(-1, 4, 4, own, 16 * own).transpose(0, 2, 1, 3, 4).reshape(hot_a.shape)
    scaling = 1.0 / math.sqrt(own * 16)
    cross = cross_products(
        hot_a, hot_b, english, (p0, p1, p2, p3), (q0, q1, q2, q3), scaling
    )
    return ffn_out, cross


def solution(mesh):
    in_specs = (P("feat", None, "tok"), P("tok", "feat"), P("tok", "feat"), P("feat", "tok"), P())
    out_specs = (P("feat", None, "tok"), P(None, "feat", "tok"))
    small = mesh.shape["feat"] == 16 and mesh.shape["tok"] == 2
    body = on_small if small else on_any
    return jax.shard_map(
        body, mesh=mesh, in_specs=in_specs, out_specs=out_specs, check_vma=False
    )
```

```python
import math

import jax
import jax.numpy as jnp
import numpy as np
from jax import lax
from jax.experimental import pallas as pl
from jax.experimental.pallas import tpu as pltpu
from jax.sharding import PartitionSpec as P

BF16 = jnp.bfloat16
F32 = jnp.float32


def feat_shape(n):
    if n == 16:
        return 4, 2, 2
    if n == 32:
        return 2, 4, 4
    return 1, 1, n


def folded(n):
    return list(range(0, n, 2)) + list(range(1, n, 2))[::-1]


def plane_cycle(ny, nx):
    if ny < 2 or nx < 2:
        return folded(ny * nx)
    cycle = [(0, x) for x in range(nx)]
    for y in range(1, ny):
        xs = range(1, nx) if y % 2 == 0 else range(nx - 1, 0, -1)
        cycle += [(y, x) for x in xs]
    cycle += [(y, 0) for y in range(ny - 1, 0, -1)]
    return [y * nx + x for y, x in cycle]


class Rings:
    def __init__(self, n_feat, n_tok):
        nz, ny, nx = feat_shape(n_feat)
        self.n_feat, self.n_tok = n_feat, n_tok
        self.nz, self.npl = nz, ny * nx
        self.zorder = folded(nz)
        self.porder = plane_cycle(ny, nx)
        self.zpos = {z: i for i, z in enumerate(self.zorder)}
        self.ppos = {p: i for i, p in enumerate(self.porder)}

    def source(self, f, t, j, i):
        sign = 1 if t % 2 == 0 else -1
        z, p = divmod(f, self.npl)
        z2 = self.zorder[(self.zpos[z] - i) % self.nz]
        p2 = self.porder[(self.ppos[p] - sign * j) % self.npl]
        return z2 * self.npl + p2

    def perm(self, which, back):
        pairs = []
        for f in range(self.n_feat):
            for t in range(self.n_tok):
                j, i = (1, 0) if which == "p" else (0, 1)
                s = self.source(f, t, j, i)
                pair = (s * self.n_tok + t, f * self.n_tok + t)
                pairs.append(pair[::-1] if back else pair)
        return sorted(pairs)

    def size(self, which):
        return self.npl if which == "p" else self.nz

    def step(self, x, which, back=False):
        return lax.ppermute(x, ("feat", "tok"), self.perm(which, back))

    def gather(self, a, b, wa, wb):
        a, b = [a], [b]
        for k in range(1, max(self.size(wa), self.size(wb))):
            if k < self.size(wa):
                a.append(self.step(a[-1], wa))
            if k < self.size(wb):
                b.append(self.step(b[-1], wb))
            a[-1], b[-1] = lax.optimization_barrier((a[-1], b[-1]))
        return a, b

    def scatter(self, parts_a, parts_b, wa, wb, source):
        ja, jb = self.size(wa) - 1, self.size(wb) - 1
        a, b = parts_a(source, ja), parts_b(source, jb)
        while ja or jb:
            a, b, source = lax.optimization_barrier((a, b, source))
            got = [self.step(a, wa, True) if ja else a, self.step(b, wb, True) if jb else b]
            more = [parts_a(source, ja - 1) if ja else None, parts_b(source, jb - 1) if jb else None]
            got, more = lax.optimization_barrier((got, more))
            a, b = (
                g if m is None else (g.astype(F32) + m.astype(F32)).astype(BF16)
                for g, m in zip(got, more)
            )
            ja, jb = max(ja - 1, 0), max(jb - 1, 0)
        return a, b


def mirror(n):
    return [(n - j) % n for j in range(n)]


def on_any(tokens, gate_weight, up_weight, down_weight, alignment):
    n_feat, n_tok = lax.axis_size("feat"), lax.axis_size("tok")
    rings = Rings(n_feat, n_tok)
    nz, npl = rings.nz, rings.npl
    own, langs, width = tokens.shape
    rows = own * langs
    hid = gate_weight.shape[1]
    f, t = lax.axis_index("feat"), lax.axis_index("tok")
    cut = max(width * 21 // 32 // 128 * 128, 128)

    x = tokens.transpose(1, 0, 2).reshape(rows, width)

    a, b = rings.gather(x[:, :cut], x[:, cut:], "z", "p")
    a, b = rings.gather(jnp.concatenate(a, 0), jnp.concatenate(b, 0), "p", "z")
    a, b = jnp.concatenate(a, 0), jnp.concatenate(b, 0)
    b = b.reshape(nz, npl, rows, width - cut).transpose(1, 0, 2, 3).reshape(-1, width - cut)
    full = jnp.concatenate((a, b), 1)

    gate = jnp.dot(full, gate_weight, preferred_element_type=F32).astype(BF16)
    up = jnp.dot(full, up_weight, preferred_element_type=F32).astype(BF16)

    def over_tok(v):
        v = v.reshape(npl, nz * rows, hid)
        flip = [v[j] for j in mirror(npl)]
        if n_tok == 2:
            other = lax.ppermute(v, "tok", [(0, 1), (1, 0)])
            other = jnp.stack([other[j] for j in mirror(npl)])
            return v.astype(F32) + other.astype(F32)
        odd = t % 2 == 1
        v = jnp.where(odd, jnp.stack(flip), v)
        total = lax.psum(v, "tok").astype(F32)
        return jnp.where(odd, jnp.stack([total[j] for j in mirror(npl)]), total)

    hidden = (jax.nn.silu(over_tok(gate)) * over_tok(up)).astype(BF16)
    hidden = hidden.reshape(-1, hid)

    def down_a(h, j):
        h = h.reshape(npl, -1, hid)[j]
        return jnp.dot(h, down_weight[:, :cut], preferred_element_type=F32).astype(BF16)

    def down_b(h, i):
        h = h.reshape(npl, nz, rows, hid)[:, i].reshape(-1, hid)
        return jnp.dot(h, down_weight[:, cut:], preferred_element_type=F32).astype(BF16)

    oa, ob = rings.scatter(down_a, down_b, "p", "z", hidden)
    oa, ob = oa.reshape(nz, rows, cut), ob.reshape(npl, rows, width - cut)
    oa, ob = rings.scatter(lambda s, j: s[0][j], lambda s, j: s[1][j], "z", "p", (oa, ob))

    ffn_out = jnp.concatenate((oa, ob), 1).reshape(langs, own, width).transpose(1, 0, 2)

    a, b = oa.reshape(langs, own, cut), ob.reshape(langs, own, width - cut)
    a, b = rings.gather(a, b, "z", "p")
    a = jnp.stack(a, 1).reshape(langs, nz * own, cut)
    b = jnp.stack(b, 1).reshape(langs, npl * own, width - cut)
    a, b = rings.gather(a, b, "p", "z")
    a = jnp.stack(a, 1).reshape(langs, -1, cut)
    b = jnp.stack(b, 1)
    b = b.reshape(langs, nz, npl, own, width - cut).transpose(0, 2, 1, 3, 4)
    b = b.reshape(langs, -1, width - cut)
    out_all = jnp.concatenate((a, b), 2)

    ids = np.zeros((n_feat, n_tok, npl, nz, own), np.int32)
    for ff in range(n_feat):
        for tt in range(n_tok):
            for j in range(npl):
                for i in range(nz):
                    ids[ff, tt, j, i] = rings.source(ff, tt, j, i) * own + np.arange(own)
    ids = jnp.asarray(ids.reshape(n_feat * n_tok, -1))
    mine = lax.dynamic_index_in_dim(ids, f * n_tok + t, 0, keepdims=False)

    ratio = n_feat // n_tok
    fw = width // ratio
    own_block = lax.dynamic_slice_in_dim(out_all[0], f % ratio * fw, fw, 1)
    root = f // ratio
    if n_tok == 2:
        other = lax.ppermute(own_block, "tok", [(0, 1), (1, 0)])
        other = other.reshape(npl, nz * own, fw)
        other = jnp.stack([other[j] for j in mirror(npl)]).reshape(-1, fw)
        english = jnp.where(root == t, own_block, other)
    else:
        def flip(v):
            v = v.reshape(npl, nz * own, fw)
            return jnp.stack([v[j] for j in mirror(npl)]).reshape(-1, fw)

        odd = t % 2 == 1
        block = jnp.where(odd, flip(own_block), own_block)
        block = lax.psum(jnp.where(root == t, block, jnp.zeros_like(block)), "tok")
        english = jnp.where(odd, flip(block), block)

    targets = jnp.take(alignment, mine, axis=1)
    onehot = (mine[None, :, None] == targets[:, None, :]).astype(BF16)
    moved = jnp.einsum("lri,ic->lrc", onehot, english, preferred_element_type=F32).astype(BF16)
    scaling = 1.0 / math.sqrt(own * n_feat)
    cross = jnp.einsum("lrc,lrd->lcd", moved, out_all[1:], preferred_element_type=F32) * scaling
    return ffn_out, cross


class Small:
    def __init__(self):
        self.rings = Rings(16, 2)

    def mask(self, slot, t):
        one, two = slot & 1, slot >> 1
        return one + 2 * two if t == 0 else 2 * one + two

    def plane(self, x, slot):
        pairs = [(2 * f + t, 2 * (f ^ self.mask(slot, t)) + t) for f in range(16) for t in range(2)]
        return lax.ppermute(x, ("feat", "tok"), pairs)

    def z(self, x, slot=1, back=False):
        pairs = []
        for f in range(16):
            for t in range(2):
                pair = (2 * self.rings.source(f, t, 0, slot) + t, 2 * f + t)
                pairs.append(pair[::-1] if back else pair)
        return lax.ppermute(x, ("feat", "tok"), sorted(pairs))

    def tokens(self, own):
        ids = np.zeros((16, 2, 4, 4, own), np.int32)
        for f in range(16):
            for t in range(2):
                for p in range(4):
                    for i in range(4):
                        source = self.rings.source(f ^ self.mask(p, t), t, 0, i)
                        ids[f, t, p, i] = source * own + np.arange(own)
        return ids.reshape(32, -1)


def total(*parts):
    return sum(p.astype(F32) for p in parts).astype(BF16)


def early_kernel(gate_weight, up_weight, x, gate, up):
    gate[...] = jnp.dot(x[...], gate_weight[...], preferred_element_type=F32)
    up[...] = jnp.dot(x[...], up_weight[...], preferred_element_type=F32)


def late_kernel(gate_weight, up_weight, *refs):
    mids, a3, b, (gate, up, x) = refs[:6], refs[6], refs[7:11], refs[11:]
    block, cut = a3.shape
    rows = block // 4

    @pl.when(pl.program_id(0) == 0)
    def _():
        for p in range(4):
            for i in range(4):
                start = p * block + i * rows
                x[start:start + rows, :] = b[i][p * rows:(p + 1) * rows, :]

    for weight, mid, out in ((gate_weight, mids[::2], gate), (up_weight, mids[1::2], up)):
        more = jnp.dot(x[...], weight[cut:, :], preferred_element_type=F32)
        last = jnp.dot(a3[...], weight[:cut, :], preferred_element_type=F32)
        start = 0
        for part in [*mid, last]:
            end = start + part.shape[0]
            out[start:end, :] = (more[start:end] + part[...]).astype(BF16)
            start = end


TILE = 256


def early_products(x, gate_weight, up_weight):
    rows, cut = x.shape
    hid = gate_weight.shape[1]
    weight = pl.BlockSpec((cut, TILE), lambda n: (0, n))
    out = pl.BlockSpec((rows, TILE), lambda n: (0, n))
    return pl.pallas_call(
        early_kernel,
        grid=(hid // TILE,),
        in_specs=[weight] * 2 + [pl.BlockSpec(memory_space=pltpu.VMEM)],
        out_specs=[out] * 2,
        out_shape=[jax.ShapeDtypeStruct((rows, hid), F32)] * 2,
        compiler_params=pltpu.CompilerParams(
            dimension_semantics=("arbitrary",), vmem_limit_bytes=7 << 20
        ),
    )(gate_weight, up_weight, x)


def late_products(mids, a3, b, gate_weight, up_weight, first, count):
    width = gate_weight.shape[0]
    block = a3.shape[0]
    weight = pl.BlockSpec((width, TILE), lambda n: (0, n + first))
    mid = [pl.BlockSpec((m.shape[0], TILE), lambda n: (0, n + first)) for m in mids]
    out = pl.BlockSpec((4 * block, TILE), lambda n: (0, n))
    return pl.pallas_call(
        late_kernel,
        grid=(count,),
        in_specs=[weight] * 2 + mid + [pl.BlockSpec(memory_space=pltpu.VMEM)] * 5,
        out_specs=[out] * 2,
        out_shape=[jax.ShapeDtypeStruct((4 * block, count * TILE), BF16)] * 2,
        scratch_shapes=[pltpu.VMEM((4 * block, b[0].shape[1]), BF16)],
        compiler_params=pltpu.CompilerParams(
            dimension_semantics=("arbitrary",), vmem_limit_bytes=12 << 20
        ),
    )(gate_weight, up_weight, *mids, a3, *b)


def cross_kernel(scaling, hot_a, hot_b, english, *refs):
    out, moved_a, moved_b = refs[8:]
    lang, step = pl.program_id(0), pl.program_id(1)
    tile = out.shape[1]

    @pl.when(step == 0)
    def _():
        for hot, moved in ((hot_a, moved_a), (hot_b, moved_b)):
            rows = jnp.dot(hot[lang], english[...], preferred_element_type=F32)
            moved[...] = rows.astype(BF16).T

    at = pl.ds(pl.multiple_of(step * tile, tile), tile)
    start = 0
    for moved, blocks in ((moved_a, refs[:4]), (moved_b, refs[4:8])):
        width = blocks[0].shape[2]
        rows = jnp.concatenate([b[lang + 1] for b in blocks], 0)
        out[0, :, start:start + width] = jnp.dot(
            moved[at, :], rows, preferred_element_type=F32
        ) * scaling
        start += width


def cross_products(hot_a, hot_b, english, a, b, scaling):
    langs, tokens, _ = hot_a.shape
    height = english.shape[1]
    width = a[0].shape[2] + b[0].shape[2]
    tile = 256
    return pl.pallas_call(
        lambda *refs: cross_kernel(scaling, *refs),
        grid=(langs, height // tile),
        in_specs=[pl.BlockSpec(memory_space=pltpu.VMEM)] * 11,
        out_specs=pl.BlockSpec((1, tile, width), lambda l, r: (l, r, 0)),
        out_shape=jax.ShapeDtypeStruct((langs, height, width), F32),
        scratch_shapes=[pltpu.VMEM((height, tokens), BF16)] * 2,
        compiler_params=pltpu.CompilerParams(
            dimension_semantics=("arbitrary", "arbitrary"), vmem_limit_bytes=12 << 20
        ),
    )(hot_a, hot_b, english, *a, *b)


def on_small(tokens, gate_weight, up_weight, down_weight, alignment):
    net = Small()
    own, langs, width = tokens.shape
    rows = own * langs
    hid = gate_weight.shape[1]
    f, t = lax.axis_index("feat"), lax.axis_index("tok")
    cut = width * 5 // 8
    lock = lax.optimization_barrier

    x = tokens.transpose(1, 0, 2).reshape(rows, width)

    a, b = x[:, :cut], x[:, cut:]
    b1, a1, b2, a2, b3, a3 = (
        net.plane(b, 1), net.z(a, 1), net.plane(b, 2), net.z(a, 3), net.plane(b, 3), None
    )
    a3 = net.z(a1, 1)
    weights = [pltpu.with_memory_space_constraint(w, pltpu.HBM) for w in (gate_weight, up_weight)]
    b0 = jnp.concatenate((b, b1, b2, b3), 0)
    a0 = jnp.concatenate((a, a1, a3, a2), 0)
    a0, b0 = lock((a0, b0))
    a1, b1 = net.plane(a0, 1), net.z(b0)
    mids = early_products(a0, *weights)
    a0, a1, b1, mids = lock((a0, a1, b1, mids))
    a2, b2 = net.plane(a0, 2), net.z(b1)
    mids += early_products(a1, *weights)
    a0, a1, a2, b2, mids = lock((a0, a1, a2, b2, mids))
    a3, b3 = net.plane(a1, 2), net.z(b2)
    mids += early_products(a2, *weights)
    a3, b3, mids = lock((a3, b3, mids))

    def core(v):
        return lax.ppermute(v, "tok", [(0, 1), (1, 0)])

    def mirror(v):
        v = v.reshape(4, -1, v.shape[-1])
        return jnp.stack((v[0], v[2], v[1], v[3])).reshape(-1, v.shape[-1])

    tiles = hid // TILE
    early = tiles // 2 + 2
    hidden = []
    for first, count in ((0, early), (early, tiles - early)):
        gate, up = late_products(
            mids, a3, (b0, b1, b2, b3), *weights, first, count
        )
        gate = gate.astype(F32) + mirror(core(gate)).astype(F32)
        up = up.astype(F32) + mirror(core(up)).astype(F32)
        hidden.append((jax.nn.silu(gate) * up).astype(BF16))
    hidden = jnp.concatenate(hidden, 1)

    def down_a(h, j):
        h = h[j * 4 * rows:(j + 1) * 4 * rows]
        return jnp.dot(h, down_weight[:, :cut], preferred_element_type=F32).astype(BF16)

    def down_b(h, i):
        h = h.reshape(4, 4, rows, hid)[:, i].reshape(-1, hid)
        return jnp.dot(h, down_weight[:, cut:], preferred_element_type=F32).astype(BF16)

    p, q = down_a(hidden, 3), down_b(hidden, 3)
    p, q, hidden = lock((p, q, hidden))
    s3, r3 = net.plane(p, 2), net.z(q, back=True)
    p, q = down_a(hidden, 2), down_b(hidden, 2)
    s3, r3, p, q, hidden = lock((s3, r3, p, q, hidden))
    p, q, hidden = lock((p, total(q, r3), hidden))
    s2, r2 = net.plane(p, 2), net.z(q, back=True)
    p, q = down_a(hidden, 1), down_b(hidden, 1)
    s2, r2, p, q, hidden = lock((s2, r2, p, q, hidden))
    p, q, hidden = lock((total(p, s3), total(q, r2), hidden))
    s1, r1 = net.plane(p, 1), net.z(q, back=True)
    p, q = down_a(hidden, 0), down_b(hidden, 0)
    s1, r1, p, q = lock((s1, r1, p, q))
    p = total(p, s1, s2).reshape(4, rows, cut)
    q = total(q, r1).reshape(4, rows, width - cut)
    p, q = lock((p, q))
    r1, r2, r3, g1, g3, g2 = lock((
        net.plane(q[1], 1), net.plane(q[2], 2), net.plane(q[3], 3),
        net.z(p[1], 1, True), net.z(p[3], 3, True), net.z(p[2], 2, True),
    ))
    p, q = lock((total(p[0], g1, g2, g3), total(q[0], r1, r2, r3)))

    ffn_out = jnp.concatenate((p, q), 1).reshape(langs, own, width).transpose(1, 0, 2)

    r1, g1, r2, g3, r3 = net.plane(q, 1), net.z(p, 1), net.plane(q, 2), net.z(p, 3), net.plane(q, 3)
    g2 = net.z(g1, 1)

    def join(*v):
        v = [x.reshape(langs, own, -1) for x in v]
        return jnp.stack(v, 1).reshape(langs, 4 * own, -1)

    p0 = join(p, g1, g2, g3)
    q0 = join(q, r1, r2, r3)
    p0, q0 = lock((p0, q0))
    p0, p1, q1 = lock((p0, net.plane(p0, 1), net.z(q0)))
    p0, p1, p2, q2 = lock((p0, p1, net.plane(p0, 2), net.z(q1)))
    p3, q3 = lock((net.plane(p1, 2), net.z(q2)))

    ea = jnp.concatenate((p0[0], p1[0], p2[0], p3[0]), 0)
    eb = jnp.stack((q0[0], q1[0], q2[0], q3[0])).reshape(4, 4, own, width - cut)
    eb = eb.transpose(1, 0, 2, 3).reshape(-1, width - cut)
    fw = width // 8
    block = lax.dynamic_slice_in_dim(jnp.concatenate((ea, eb), 1), f % 8 * fw, fw, 1)
    english = jnp.where(f // 8 == t, block, mirror(core(block)))

    ids = jnp.asarray(net.tokens(own))
    ids = lax.dynamic_index_in_dim(ids, f * 2 + t, 0, keepdims=False)
    targets = jnp.take(alignment, ids, axis=1)
    hot_a = (ids[None, :, None] == targets[:, None, :]).astype(BF16)
    hot_b = hot_a.reshape(-1, 4, 4, own, 16 * own).transpose(0, 2, 1, 3, 4).reshape(hot_a.shape)
    scaling = 1.0 / math.sqrt(own * 16)
    cross = cross_products(
        hot_a, hot_b, english, (p0, p1, p2, p3), (q0, q1, q2, q3), scaling
    )
    return ffn_out, cross


def solution(mesh):
    in_specs = (P("feat", None, "tok"), P("tok", "feat"), P("tok", "feat"), P("feat", "tok"), P())
    out_specs = (P("feat", None, "tok"), P(None, "feat", "tok"))
    small = mesh.shape["feat"] == 16 and mesh.shape["tok"] == 2
    body = on_small if small else on_any
    return jax.shard_map(
        body, mesh=mesh, in_specs=in_specs, out_specs=out_specs, check_vma=False
    )
```
